32 devices in a mesh: row: 8 (over y, x, core), col: 4 (over z).
Axes of the slice: x: 2, y: 2, z: 4, core: 2. Of those that a mesh axis runs over, the one named last changes fastest.
Arguments:
- left_act: bfloat16 [32, 64, 256], P(None, 'col', 'row'), may hold values from -6 to 6
- right_act: bfloat16 [32, 64, 256], P(None, 'row', 'col'), may hold values from -6 to 6
- cotangent: bfloat16 [256, 256, 128], P('row', 'col'), may hold values from -4 to 4
- weight: bfloat16 [1024, 128], replicated, may hold values from -0.1875 to 0.1875
Outputs:
- grad_left: float32 [32, 64, 256], P(None, 'col', 'row')
- grad_right: float32 [32, 64, 256], P(None, 'row', 'col')
- grad_weight: float32 [1024, 128], P('row')
The draws below stay inside these ranges and needn't reach their ends.
All inputs are finite; a program needn't handle non-finite values.
Results may differ from the reference program's by a relative error of at most 0.0029.
Values may be sent and summed in bfloat16 or wider, within the bound.
No kernel may reach another device: no remote copies, remote signals or barrier semaphores. Data moves between devices by JAX's collectives and lax.ppermute only.
A program may use at most 128 MiB of HBM per device.

```python
import jax
import jax.numpy as jnp
from jax import lax

C = 32
E = 128
S = 64
TI = 32
TOKENS = 256


def levels(own_key, shape, cuts, least, high):
    def one(position, shards_of):
        steps = jax.random.uniform(jax.random.fold_in(jax.random.fold_in(own_key, 6), position), (shards_of,), jnp.float32, least / len(cuts), high / len(cuts))
        return jnp.repeat(jnp.exp(steps), shape[position] // shards_of).reshape((-1,) + (1,) * (len(shape) - position - 1))

    gain = one(*cuts[0])
    for cut in cuts[1:]:
        gain = gain * one(*cut)
    return gain


def centred(key, dims, deviation, most, shards=(), kind=jnp.bfloat16):
    array = jax.random.normal(key, dims, jnp.float32) * deviation
    if len(shards) > 0:
        array = levels(key, dims, shards, -0.22, 0.18) * array
    return jnp.clip(array, min=-most, max=most).astype(kind)


def setup_inputs(seed: int = 0) -> dict:
    key_list = jax.random.split(jax.random.key(seed), 5)
    return {
        "left_act": centred(key_list[0], (C, S, TOKENS), 1.0, 6.0, ((1, 4), (2, 8))),
        "right_act": centred(key_list[1], (C, S, TOKENS), 1.0, 6.0, ((1, 8), (2, 4))),
        "cotangent": centred(key_list[2], (TOKENS, TOKENS, E), 0.5, 4.0, ((0, 8), (1, 4))),
        "weight": centred(key_list[3], (C * C, E), (C * C) ** -0.5, 0.1875),
    }


def reference(left_act, right_act, cotangent, weight):
    blocks = TOKENS // TI
    left = left_act.astype(jnp.float32).reshape(C, S, blocks, TI).transpose(2, 0, 1, 3)
    grads = cotangent.reshape(blocks, TI, TOKENS, E)
    right = right_act.astype(jnp.float32)

    def step(carry, item):
        grad_w, grad_r = carry
        left_blk, grad_blk = item
        outer = (jnp.einsum('csi,dsj->ijcd', left_blk, right) / S).astype(jnp.bfloat16)
        outer_flat = outer.reshape(TI * TOKENS, C * C)
        grad_flat = grad_blk.reshape(TI * TOKENS, E)
        grad_w = grad_w + jnp.dot(outer_flat.T, grad_flat, preferred_element_type=jnp.float32)
        grad_outer = jnp.dot(grad_flat, weight.T, preferred_element_type=jnp.float32).astype(jnp.bfloat16)
        grad_outer = grad_outer.reshape(TI, TOKENS, C, C).astype(jnp.float32)
        grad_l = jnp.einsum('ijcd,dsj->csi', grad_outer, right) / S
        grad_r = grad_r + jnp.einsum('ijcd,csi->dsj', grad_outer, left_blk) / S
        return (grad_w, grad_r), grad_l

    start = (jnp.zeros((C * C, E), jnp.float32), jnp.zeros((C, S, TOKENS), jnp.float32))
    (grad_weight, grad_right), pieces = lax.scan(step, start, (left, grads))
    grad_left = pieces.transpose(1, 2, 0, 3).reshape(C, S, TOKENS)
    return grad_left, grad_right, grad_weight
```

```python
import functools

import jax
import jax.numpy as jnp
from jax import lax
from jax.experimental import pallas as pl
from jax.experimental.pallas import tpu as pltpu
from jax.sharding import PartitionSpec as P


F32 = jnp.float32
BF16 = jnp.bfloat16
STEPS = 4


def xor_permute(x, axis, size, k):
    return lax.ppermute(x, axis, [(r, r ^ k) for r in range(size)])


def fill_pairs(g_ref, gbd_ref, first):
    per, tj, e = g_ref.shape

    @pl.when(first)
    def _():
        gbd_ref[...] = jnp.zeros_like(gbd_ref)

    for i in range(per):
        block = g_ref[i]
        gbd_ref[2 * i * tj : (2 * i + 1) * tj, :e] = block
        gbd_ref[(2 * i + 1) * tj : (2 * i + 2) * tj, e:] = block


def outer_grad_kernel(g_ref, w_ref, y_ref, gbd_ref):
    per, tj, _ = g_ref.shape
    pairs = y_ref.shape[1] // (2 * tj)
    chans = w_ref.shape[0] // pairs
    lanes = 2 * tj
    fill_pairs(g_ref, gbd_ref, pl.program_id(0) == 0)
    group = 4
    for first in range(0, pairs, group):
        res = lax.dot_general(
            w_ref[first * chans : (first + group) * chans, :],
            gbd_ref[...],
            (((1,), (1,)), ((), ())),
            preferred_element_type=F32,
        ).astype(BF16)
        for p in range(group):
            for i in range(per):
                y_ref[
                    i * chans : (i + 1) * chans,
                    (first + p) * lanes : (first + p + 1) * lanes,
                ] = res[p * chans : (p + 1) * chans, i * lanes : (i + 1) * lanes]


def main_kernel(n_row, n_col, total, *refs):
    chips = n_row // 2
    l_refs = refs[:n_col]
    r_refs = refs[n_col : n_col + chips]
    other_ref, g_ref, y_ref = refs[n_col + chips : n_col + chips + 3]
    keep_ref, send_ref, l_out = refs[n_col + chips + 3 : n_col + chips + 6]
    lblk, rblk, l_all, r_all, gbd, x_ref, w_acc, r_acc, l_acc, part = refs[n_col + chips + 6 :]
    step = pl.program_id(0)
    row = lax.axis_index("row")
    col = lax.axis_index("col")
    core = row % 2
    chip = row // 2
    per, tj, e = g_ref.shape
    s_r, wide = r_refs[0].shape
    s_l = l_refs[0].shape[0]
    rows = y_ref.shape[0]
    chans = rows // per
    lanes = 2 * tj
    pairs = wide // lanes

    @pl.when(step == 0)
    def _():
        for k in range(n_col):
            lblk[k] = l_refs[k][...]
        for k in range(chips):
            rblk[k] = r_refs[k][...]
            rblk[chips + k] = other_ref[k]
        l_all[...] = jnp.concatenate([lblk[p ^ col] for p in range(n_col)], axis=0)
        r_all[...] = jnp.concatenate(
            [rblk[((p % 2) ^ core) * chips + ((p // 2) ^ chip)] for p in range(n_row)], axis=0
        )

    fill_pairs(g_ref, gbd, step == 0)
    left = l_all[:, pl.ds(pl.multiple_of(step * rows, rows), rows)]
    group = 4
    for first in range(0, pairs, group):
        res = lax.dot_general(
            left,
            r_all[:, first * lanes : (first + group) * lanes],
            (((0,), (0,)), ((), ())),
            preferred_element_type=F32,
        ).astype(BF16)
        for p in range(group):
            for i in range(per):
                x_ref[
                    (first + p) * chans : (first + p + 1) * chans, i * lanes : (i + 1) * lanes
                ] = res[i * chans : (i + 1) * chans, p * lanes : (p + 1) * lanes]
    w_new = jnp.dot(x_ref[...], gbd[...], preferred_element_type=F32)
    r_new = jnp.dot(left, y_ref[...], preferred_element_type=F32)
    l_acc[:, pl.ds(pl.multiple_of(step * rows, rows), rows)] = lax.dot_general(
        r_all[...], y_ref[...], (((1,), (1,)), ((), ())), preferred_element_type=F32
    )

    @pl.when(step == 0)
    def _():
        w_acc[...] = w_new
        r_acc[...] = r_new

    @pl.when(step > 0)
    def _():
        w_acc[...] += w_new
        r_acc[...] += r_new

    @pl.when(step == STEPS - 1)
    def _():
        scale = 1.0 / total
        own_c = chans // n_row
        for r in range(n_row):
            part[r, :s_r, :] = r_acc[r * s_r : (r + 1) * s_r, :] * scale
            piece = jnp.concatenate(
                [w_acc[p * chans + r * own_c : p * chans + (r + 1) * own_c, :] for p in range(pairs)],
                axis=0,
            )
            w_rows = piece.shape[0] * piece.shape[1] // wide
            fold = wide // piece.shape[1]
            part[r, s_r : s_r + w_rows, :] = (
                jnp.concatenate(
                    [piece[a * w_rows : (a + 1) * w_rows, :] for a in range(fold)], axis=1
                )
                * scale
            )
        for k in range(chips):
            keep_ref[k] = part[2 * (chip ^ k) + core]
            send_ref[k] = part[2 * (chip ^ k) + 1 - core]
        for p in range(n_col):
            l_out[p ^ col] = l_acc[p * s_l : (p + 1) * s_l, :] * scale


def body(n_row, n_col, left_act, right_act, cotangent, weight):
    chans, s_l, ti = left_act.shape
    _, s_r, tj = right_act.shape
    e = cotangent.shape[2]
    chips = n_row // 2
    total = s_l * n_col
    pairs = chans // 2
    wide = chans * tj
    tall = chans * ti
    per = ti // STEPS
    rows = per * chans

    l_own = left_act.transpose(1, 2, 0).reshape(s_l, tall)
    r_own = right_act.transpose(1, 0, 2).reshape(s_r, wide)
    r_set = [r_own] + [xor_permute(r_own, "row", n_row, 2 * k) for k in range(1, chips)]
    l_set = [l_own] + [xor_permute(l_own, "col", n_col, k) for k in range(1, n_col)]
    r_other = xor_permute(jnp.stack(r_set), "row", n_row, 1)

    w_pairs = weight.reshape(chans, pairs, 2, e).transpose(1, 0, 2, 3).reshape(pairs * chans, 2 * e)
    y = pl.pallas_call(
        outer_grad_kernel,
        grid=(STEPS,),
        in_specs=[
            pl.BlockSpec((per, tj, e), lambda g: (g, 0, 0)),
            pl.BlockSpec((pairs * chans, 2 * e), lambda g: (0, 0)),
        ],
        out_specs=pl.BlockSpec((rows, wide), lambda g: (g, 0)),
        out_shape=jax.ShapeDtypeStruct((tall, wide), BF16),
        scratch_shapes=[pltpu.VMEM((2 * per * tj, 2 * e), BF16)],
        cost_estimate=pl.CostEstimate(
            flops=4 * ti * tj * e * chans * chans, bytes_accessed=6 << 20, transcendentals=0
        ),
    )(cotangent, w_pairs)

    w_rows = chans * chans * e // n_row // wide
    high = s_r + w_rows
    whole = lambda *shape: pl.BlockSpec(shape, lambda g: (0,) * len(shape))
    keep, send, l_part = pl.pallas_call(
        functools.partial(main_kernel, n_row, n_col, total),
        grid=(STEPS,),
        in_specs=[whole(s_l, tall)] * n_col
        + [whole(s_r, wide)] * chips
        + [
            whole(chips, s_r, wide),
            pl.BlockSpec((per, tj, e), lambda g: (g, 0, 0)),
            pl.BlockSpec((rows, wide), lambda g: (g, 0)),
        ],
        out_specs=[whole(chips, high, wide), whole(chips, high, wide), whole(n_col, s_l, tall)],
        out_shape=[
            jax.ShapeDtypeStruct((chips, high, wide), F32),
            jax.ShapeDtypeStruct((chips, high, wide), F32),
            jax.ShapeDtypeStruct((n_col, s_l, tall), F32),
        ],
        scratch_shapes=[
            pltpu.VMEM((n_col, s_l, tall), BF16),
            pltpu.VMEM((n_row, s_r, wide), BF16),
            pltpu.VMEM((total, tall), BF16),
            pltpu.VMEM((total, wide), BF16),
            pltpu.VMEM((2 * per * tj, 2 * e), BF16),
            pltpu.VMEM((pairs * chans, 2 * per * tj), BF16),
            pltpu.VMEM((pairs * chans, 2 * e), F32),
            pltpu.VMEM((total, wide), F32),
            pltpu.VMEM((total, tall), F32),
            pltpu.VMEM((n_row, high, wide), F32),
        ],
    )(*l_set, *r_set, r_other, cotangent, y)

    summed = keep + xor_permute(send, "row", n_row, 1)
    got = [xor_permute(summed[k].astype(BF16), "row", n_row, 2 * k) for k in range(1, chips)]
    row_sum = summed[0]
    for item in got:
        row_sum = row_sum + item.astype(F32)
    grad_right = row_sum[:s_r].reshape(s_r, chans, tj).transpose(1, 0, 2)

    w_own = row_sum[s_r:].astype(BF16)
    l_half = l_part.reshape(n_col, s_l, tall)
    sums_l = l_half[0]
    outs = [
        (
            xor_permute(l_half[k].astype(BF16), "col", n_col, k),
            xor_permute(w_own, "col", n_col, k),
        )
        for k in range(1, n_col)
    ]
    for item, _ in outs:
        sums_l = sums_l + item.astype(F32)
    grad_left = sums_l.reshape(s_l, ti, chans).transpose(2, 0, 1)
    tree = [w_own.astype(F32)] + [item.astype(F32) for _, item in outs]
    while len(tree) > 1:
        tree = [tree[a] + tree[a + 1] for a in range(0, len(tree), 2)]
    own_c = chans // n_row
    fold = wide // (2 * e)
    grad_weight = tree[0].reshape(w_rows, fold, 2, e).transpose(1, 0, 2, 3)
    grad_weight = (
        grad_weight.reshape(pairs, own_c, 2, e).transpose(1, 0, 2, 3).reshape(own_c * chans, e)
    )
    return grad_left, grad_right, grad_weight


def solution(mesh):
    return jax.shard_map(
        functools.partial(body, mesh.shape["row"], mesh.shape["col"]),
        mesh=mesh,
        in_specs=(P(None, "col", "row"), P(None, "row", "col"), P("row", "col", None), P()),
        out_specs=(P(None, "col", "row"), P(None, "row", "col"), P("row", None)),
        check_vma=False,
    )
```

```python
import functools

import jax
import jax.numpy as jnp
from jax import lax
from jax.experimental import pallas as pl
from jax.experimental.pallas import tpu as pltpu
from jax.sharding import PartitionSpec as P


F32 = jnp.float32
BF16 = jnp.bfloat16
STEPS = 4
VMEM = pl.BlockSpec(memory_space=pltpu.VMEM)


def xor_permute(x, axis, size, k):
    return lax.ppermute(x, axis, [(r, r ^ k) for r in range(size)])


def chunk(step, size):
    return pl.ds(pl.multiple_of(step * size, size), size)


def outer_grad_kernel(g_ref, w_ref, y_ref, gbd_ref, w32, wp):
    ti, tj, e = g_ref.shape
    lanes = 2 * tj
    pairs = y_ref.shape[1] // lanes
    chans = 2 * pairs
    per = ti // STEPS
    w32[...] = w_ref[...].astype(F32)
    for p in range(pairs):
        for d2 in range(2):
            wp[p * chans : (p + 1) * chans, d2 * e : (d2 + 1) * e] = w32[
                pl.ds(2 * p + d2, chans, stride=chans), :
            ].astype(BF16)
    zero = jnp.zeros((tj, e), BF16)
    group = 4

    def step(s, carry):
        for i in range(per):
            block = g_ref[s * per + i]
            base = pl.multiple_of((s * per + i) * lanes, lanes)
            gbd_ref[pl.ds(base, tj), :e] = block
            gbd_ref[pl.ds(base, tj), e:] = zero
            gbd_ref[pl.ds(base + tj, tj), :e] = zero
            gbd_ref[pl.ds(base + tj, tj), e:] = block
        rhs = gbd_ref[chunk(s, per * lanes), :]
        for first in range(0, pairs, group):
            res = lax.dot_general(
                wp[first * chans : (first + group) * chans, :],
                rhs,
                (((1,), (1,)), ((), ())),
                preferred_element_type=F32,
            ).astype(BF16)
            for p in range(group):
                for i in range(per):
                    y_ref[
                        pl.ds(pl.multiple_of((s * per + i) * chans, chans), chans),
                        (first + p) * lanes : (first + p + 1) * lanes,
                    ] = res[p * chans : (p + 1) * chans, i * lanes : (i + 1) * lanes]
        return carry

    lax.fori_loop(0, STEPS, step, 0)


def main_kernel(n_row, n_col, chans, *refs):
    chips = n_row // 2
    l_refs = refs[:n_col]
    r_refs = refs[n_col : n_col + chips]
    gbd_ref, y_ref = refs[n_col + chips : n_col + chips + 2]
    outs = refs[n_col + chips + 2 :]
    keep_ref, send_ref = outs[:2]
    l_outs = outs[2 : 2 + n_col]
    lblk, rblk, l_all, r_all, x_ref, both, l_part = outs[2 + n_col :]
    row = lax.axis_index("row")
    col = lax.axis_index("col")
    core = row % 2
    chip = row // 2
    _, s_r, wide = r_refs[0].shape
    s_l, tall = l_refs[0].shape
    total = s_l * n_col
    scale = 1.0 / total
    pairs = chans // 2
    lanes = wide // pairs
    ti = tall // chans
    per = ti // STEPS
    rows = per * chans
    two_e = gbd_ref.shape[1]
    own_c = chans // n_row

    for k in range(n_col):
        lblk[k] = l_refs[k][...]
    for k in range(chips):
        rblk[2 * k] = r_refs[k][0]
        rblk[2 * k + 1] = r_refs[k][1]
    l_all[...] = jnp.concatenate([lblk[p ^ col] for p in range(n_col)], axis=0)
    r_all[...] = jnp.concatenate(
        [rblk[2 * ((p // 2) ^ chip) + ((p % 2) ^ core)] for p in range(n_row)], axis=0
    )

    group = 4

    def outer_step(s, carry):
        left = l_all[:, chunk(s, rows)]
        for first in range(0, pairs, group):
            res = lax.dot_general(
                left,
                r_all[:, first * lanes : (first + group) * lanes],
                (((0,), (0,)), ((), ())),
                preferred_element_type=F32,
            ).astype(BF16)
            for p in range(group):
                for i in range(per):
                    x_ref[
                        (first + p) * chans : (first + p + 1) * chans,
                        pl.ds(pl.multiple_of((s * per + i) * lanes, lanes), lanes),
                    ] = res[i * chans : (i + 1) * chans, p * lanes : (p + 1) * lanes]
        return carry

    lax.fori_loop(0, STEPS, outer_step, 0)

    def place(r):
        return (r % 2) ^ core, (r // 2) ^ chip

    w_rows = pairs * own_c * two_e // wide
    height = 4
    for first in range(0, pairs, height):
        res = jnp.dot(
            x_ref[first * chans : (first + height) * chans, :],
            gbd_ref[...],
            preferred_element_type=F32,
        ) * scale
        for r in range(n_row):
            piece = jnp.concatenate(
                [
                    res[p * chans + r * own_c : p * chans + (r + 1) * own_c, :]
                    for p in range(height)
                ],
                axis=0,
            )
            side, slot = place(r)
            for a in range(height * own_c // w_rows):
                at = first * own_c // w_rows + a
                both[side, slot, s_r : s_r + w_rows, at * two_e : (at + 1) * two_e] = piece[
                    a * w_rows : (a + 1) * w_rows, :
                ]

    span = wide // 4
    for n in range(4):
        res = (
            jnp.dot(
                l_all[...], y_ref[:, n * span : (n + 1) * span], preferred_element_type=F32
            )
            * scale
        )
        for r in range(n_row):
            side, slot = place(r)
            both[side, slot, :s_r, n * span : (n + 1) * span] = res[r * s_r : (r + 1) * s_r, :]
    span = tall // 4
    for n in range(4):
        res = (
            lax.dot_general(
                r_all[...],
                y_ref[n * span : (n + 1) * span, :],
                (((1,), (1,)), ((), ())),
                preferred_element_type=F32,
            )
            * scale
        )
        for p in range(n_col):
            l_part[p ^ col, :, n * span : (n + 1) * span] = res[p * s_l : (p + 1) * s_l, :]

    keep_ref[...] = both[0]
    send_ref[...] = both[1]
    for k in range(n_col):
        l_outs[k][...] = l_part[k].astype(l_outs[k].dtype)


def body(n_row, n_col, left_act, right_act, cotangent, weight):
    chans, s_l, ti = left_act.shape
    _, s_r, tj = right_act.shape
    e = cotangent.shape[2]
    chips = n_row // 2
    total = s_l * n_col
    pairs = chans // 2
    wide = chans * tj
    tall = chans * ti

    r_own = right_act.transpose(1, 0, 2).reshape(s_r, wide)
    r_pair = jnp.stack([r_own, xor_permute(r_own, "row", n_row, 1)])
    l_own = left_act.transpose(1, 2, 0).reshape(s_l, tall)
    r_set = [r_pair] + [xor_permute(r_pair, "row", n_row, 2 * k) for k in range(1, chips)]
    l_set = [l_own] + [xor_permute(l_own, "col", n_col, k) for k in range(1, n_col)]

    y, gbd = pl.pallas_call(
        outer_grad_kernel,
        in_specs=[VMEM, VMEM],
        out_specs=[VMEM, VMEM],
        out_shape=[
            jax.ShapeDtypeStruct((tall, wide), BF16),
            jax.ShapeDtypeStruct((2 * ti * tj, 2 * e), BF16),
        ],
        scratch_shapes=[
            pltpu.VMEM((chans * chans, e), F32),
            pltpu.VMEM((pairs * chans, 2 * e), BF16),
        ],
        compiler_params=pltpu.CompilerParams(vmem_limit_bytes=16 << 20),
        cost_estimate=pl.CostEstimate(
            flops=4 * ti * tj * e * chans * chans, bytes_accessed=8 << 20, transcendentals=0
        ),
    )(cotangent, weight)

    w_rows = chans * chans * e // n_row // wide
    high = s_r + w_rows
    keep, send, *l_parts = pl.pallas_call(
        functools.partial(main_kernel, n_row, n_col, chans),
        in_specs=[VMEM] * (n_col + chips + 2),
        out_specs=[VMEM] * (2 + n_col),
        out_shape=[jax.ShapeDtypeStruct((chips, high, wide), F32)] * 2
        + [jax.ShapeDtypeStruct((s_l, tall), F32)]
        + [jax.ShapeDtypeStruct((s_l, tall), BF16)] * (n_col - 1),
        scratch_shapes=[
            pltpu.VMEM((n_col, s_l, tall), BF16),
            pltpu.VMEM((n_row, s_r, wide), BF16),
            pltpu.VMEM((total, tall), BF16),
            pltpu.VMEM((total, wide), BF16),
            pltpu.VMEM((pairs * chans, 2 * ti * tj), BF16),
            pltpu.VMEM((2, chips, high, wide), F32),
            pltpu.VMEM((n_col, s_l, tall), F32),
        ],
        compiler_params=pltpu.CompilerParams(vmem_limit_bytes=24 << 20),
    )(*l_set, *r_set, gbd, y)

    summed = keep + xor_permute(send, "row", n_row, 1)
    got = [xor_permute(summed[k].astype(BF16), "row", n_row, 2 * k) for k in range(1, chips)]
    row_sum = summed[0]
    for item in got:
        row_sum = row_sum + item.astype(F32)
    grad_right = row_sum[:s_r].reshape(s_r, chans, tj).transpose(1, 0, 2)

    w_own = row_sum[s_r:].astype(BF16)
    l_got = [xor_permute(l_parts[k], "col", n_col, k) for k in range(1, n_col)]
    w_got = [xor_permute(w_own, "col", n_col, k) for k in range(1, n_col)]
    sums_l = l_parts[0]
    for item in l_got:
        sums_l = sums_l + item.astype(F32)
    grad_left = sums_l.reshape(s_l, ti, chans).transpose(2, 0, 1)
    tree = [item.astype(F32) for item in [w_own] + w_got]
    while len(tree) > 1:
        tree = [tree[a] + tree[a + 1] for a in range(0, len(tree), 2)]
    own_c = chans // n_row
    fold = wide // (2 * e)
    grad_weight = tree[0].reshape(w_rows, fold, 2, e).transpose(1, 0, 2, 3)
    grad_weight = (
        grad_weight.reshape(pairs, own_c, 2, e).transpose(1, 0, 2, 3).reshape(own_c * chans, e)
    )
    return grad_left, grad_right, grad_weight


def solution(mesh):
    return jax.shard_map(
        functools.partial(body, mesh.shape["row"], mesh.shape["col"]),
        mesh=mesh,
        in_specs=(P(None, "col", "row"), P(None, "row", "col"), P("row", "col", None), P()),
        out_specs=(P(None, "col", "row"), P(None, "row", "col"), P("row", None)),
        check_vma=False,
    )
```

```python
import functools

import jax
import jax.numpy as jnp
from jax import lax
from jax.experimental import pallas as pl
from jax.experimental.pallas import tpu as pltpu
from jax.sharding import PartitionSpec as P


F32 = jnp.float32
BF16 = jnp.bfloat16
STEPS = 4
VMEM = pl.BlockSpec(memory_space=pltpu.VMEM)
HBM = pl.BlockSpec(memory_space=pltpu.HBM)


def xor_permute(x, axis, size, k):
    return lax.ppermute(x, axis, [(r, r ^ k) for r in range(size)])


def chunk(step, size):
    return pl.ds(pl.multiple_of(step * size, size), size)


def outer_grad_kernel(g_hbm, w_hbm, y_ref, gbd_ref, g_ref, w_ref, wp, sems):
    ti, tj, e = g_ref.shape
    lanes = 2 * tj
    pairs = y_ref.shape[1] // lanes
    chans = 2 * pairs
    per = ti // STEPS
    w_copy = pltpu.make_async_copy(w_hbm, w_ref, sems.at[STEPS])
    w_copy.start()

    def g_copy(s):
        part = pl.ds(s * per, per)
        return pltpu.make_async_copy(g_hbm.at[part], g_ref.at[part], sems.at[s])

    for s in range(STEPS):
        g_copy(s).start()
    w_copy.wait()
    swapped = jnp.swapaxes(w_ref[...].astype(F32).reshape(chans, chans, e), 0, 1).astype(BF16)
    for p in range(pairs):
        for d2 in range(2):
            wp[p * chans : (p + 1) * chans, d2 * e : (d2 + 1) * e] = swapped[2 * p + d2]
    zero = jnp.zeros((tj, e), BF16)

    def step(s, carry):
        g_copy(s).wait()
        for q in range(per // 2):
            base = (s * per + 2 * q) * lanes
            for i in range(2):
                block = g_ref[s * per + 2 * q + i]
                gbd_ref[pl.ds(base + i * lanes, tj), :e] = block
                gbd_ref[pl.ds(base + i * lanes, tj), e:] = zero
                gbd_ref[pl.ds(base + i * lanes + tj, tj), :e] = zero
                gbd_ref[pl.ds(base + i * lanes + tj, tj), e:] = block
            res = lax.dot_general(
                wp[...],
                gbd_ref[pl.ds(base, 2 * lanes), :],
                (((1,), (1,)), ((), ())),
                preferred_element_type=F32,
            ).astype(BF16)
            for i in range(2):
                at = pl.ds((s * per + 2 * q + i) * chans, chans)
                for p in range(pairs):
                    y_ref[at, p * lanes : (p + 1) * lanes] = res[
                        p * chans : (p + 1) * chans, i * lanes : (i + 1) * lanes
                    ]
        return carry

    for s in range(STEPS):
        step(s, 0)


def main_kernel(n_row, n_col, chans, *refs):
    chips = n_row // 2
    l_near, l_far = refs[:2]
    r_refs = refs[2 : 2 + chips]
    gbd_ref, y_ref, keep_ref, send_ref, l_keep, l_send = refs[2 + chips : 8 + chips]
    lblk, rblk, l_all, r_all, lt, x_ref, both, l_part = refs[8 + chips :]
    row = lax.axis_index("row")
    col = lax.axis_index("col")
    core = row % 2
    chip = row // 2
    _, s_r, wide = r_refs[0].shape
    half, s_l, tall = l_near.shape
    total = s_l * n_col
    scale = 1.0 / total
    pairs = chans // 2
    lanes = wide // pairs
    ti = tall // chans
    per = ti // STEPS
    rows = per * chans
    two_e = gbd_ref.shape[1]
    own_c = chans // n_row

    lblk[:half] = l_near[...]
    lblk[half:] = l_far[...]
    for k in range(chips):
        rblk[2 * k] = r_refs[k][0]
        rblk[2 * k + 1] = r_refs[k][1]
    l_all[...] = jnp.concatenate([lblk[p ^ col] for p in range(n_col)], axis=0)
    r_all[...] = jnp.concatenate(
        [rblk[2 * ((p // 2) ^ chip) + ((p % 2) ^ core)] for p in range(n_row)], axis=0
    )

    lt[...] = l_all[...].T
    tile = 2 * lanes

    def outer_step(n, carry):
        right = r_all[:, n * tile : (n + 1) * tile]
        for s in range(STEPS):
            res = jnp.dot(
                lt[s * rows : (s + 1) * rows, :], right, preferred_element_type=F32
            ).astype(BF16)
            for p in range(2):
                at = pl.ds((2 * n + p) * chans, chans)
                for i in range(per):
                    x_ref[at, (s * per + i) * lanes : (s * per + i + 1) * lanes] = res[
                        i * chans : (i + 1) * chans, p * lanes : (p + 1) * lanes
                    ]
        return carry

    for n in range(wide // tile):
        outer_step(n, 0)

    def place(r):
        return (r % 2) ^ core, (r // 2) ^ chip

    w_rows = pairs * own_c * two_e // wide
    height = pairs
    for first in range(0, pairs, height):
        res = jnp.dot(
            x_ref[first * chans : (first + height) * chans, :],
            gbd_ref[...],
            preferred_element_type=F32,
        ) * scale
        for r in range(n_row):
            piece = jnp.concatenate(
                [
                    res[p * chans + r * own_c : p * chans + (r + 1) * own_c, :]
                    for p in range(height)
                ],
                axis=0,
            )
            side, slot = place(r)
            for a in range(height * own_c // w_rows):
                at = first * own_c // w_rows + a
                both[side, slot, s_r : s_r + w_rows, at * two_e : (at + 1) * two_e] = piece[
                    a * w_rows : (a + 1) * w_rows, :
                ]

    span = wide // 4
    for n in range(4):
        res = (
            jnp.dot(
                l_all[...], y_ref[:, n * span : (n + 1) * span], preferred_element_type=F32
            )
            * scale
        )
        for r in range(n_row):
            side, slot = place(r)
            both[side, slot, :s_r, n * span : (n + 1) * span] = res[r * s_r : (r + 1) * s_r, :]
    span = tall // 4
    for n in range(4):
        res = (
            lax.dot_general(
                r_all[...],
                y_ref[n * span : (n + 1) * span, :],
                (((1,), (1,)), ((), ())),
                preferred_element_type=F32,
            )
            * scale
        )
        for p in range(n_col):
            l_part[p ^ col, :, n * span : (n + 1) * span] = res[p * s_l : (p + 1) * s_l, :]

    keep_ref[...] = both[0]
    send_ref[...] = both[1]
    l_keep[...] = l_part[:half]
    l_send[...] = l_part[half:].astype(BF16)


def body(n_row, n_col, left_act, right_act, cotangent, weight):
    chans, s_l, ti = left_act.shape
    _, s_r, tj = right_act.shape
    e = cotangent.shape[2]
    chips = n_row // 2
    total = s_l * n_col
    pairs = chans // 2
    wide = chans * tj
    tall = chans * ti

    r_own = right_act.transpose(1, 0, 2).reshape(s_r, wide)
    r_pair = jnp.stack([r_own, xor_permute(r_own, "row", n_row, 1)])
    l_near = left_act.transpose(1, 2, 0).reshape(1, s_l, tall)
    r_set = [r_pair] + [xor_permute(r_pair, "row", n_row, 2 * k) for k in range(1, chips)]
    half = n_col // 2
    while l_near.shape[0] < half:
        l_near = jnp.concatenate([l_near, xor_permute(l_near, "col", n_col, l_near.shape[0])])
    l_far = xor_permute(l_near, "col", n_col, half)

    y, gbd = pl.pallas_call(
        outer_grad_kernel,
        in_specs=[HBM, HBM],
        out_specs=[VMEM, VMEM],
        out_shape=[
            jax.ShapeDtypeStruct((tall, wide), BF16),
            jax.ShapeDtypeStruct((2 * ti * tj, 2 * e), BF16),
        ],
        scratch_shapes=[
            pltpu.VMEM((ti, tj, e), BF16),
            pltpu.VMEM((chans * chans, e), BF16),
            pltpu.VMEM((pairs * chans, 2 * e), BF16),
            pltpu.SemaphoreType.DMA((STEPS + 1,)),
        ],
        compiler_params=pltpu.CompilerParams(vmem_limit_bytes=16 << 20),
        cost_estimate=pl.CostEstimate(
            flops=4 * ti * tj * e * chans * chans, bytes_accessed=8 << 20, transcendentals=0
        ),
    )(
        pltpu.with_memory_space_constraint(cotangent, pltpu.HBM),
        pltpu.with_memory_space_constraint(weight, pltpu.HBM),
    )

    w_rows = chans * chans * e // n_row // wide
    high = s_r + w_rows
    keep, send, l_sum, l_send = pl.pallas_call(
        functools.partial(main_kernel, n_row, n_col, chans),
        in_specs=[VMEM] * (chips + 4),
        out_specs=[VMEM] * 4,
        out_shape=[jax.ShapeDtypeStruct((chips, high, wide), F32)] * 2
        + [jax.ShapeDtypeStruct((half, s_l, tall), kind) for kind in (F32, BF16)],
        scratch_shapes=[
            pltpu.VMEM((n_col, s_l, tall), BF16),
            pltpu.VMEM((n_row, s_r, wide), BF16),
            pltpu.VMEM((total, tall), BF16),
            pltpu.VMEM((total, wide), BF16),
            pltpu.VMEM((tall, total), BF16),
            pltpu.VMEM((pairs * chans, 2 * ti * tj), BF16),
            pltpu.VMEM((2, chips, high, wide), F32),
            pltpu.VMEM((n_col, s_l, tall), F32),
        ],
        compiler_params=pltpu.CompilerParams(vmem_limit_bytes=24 << 20),
    )(l_near, l_far, *r_set, gbd, y)

    summed = keep + xor_permute(send, "row", n_row, 1)
    got = [xor_permute(summed[k].astype(BF16), "row", n_row, 2 * k) for k in range(1, chips)]
    row_sum = summed[0]
    for item in got:
        row_sum = row_sum + item.astype(F32)
    grad_right = row_sum[:s_r].reshape(s_r, chans, tj).transpose(1, 0, 2)

    l_sum = l_sum + xor_permute(l_send, "col", n_col, half).astype(F32)
    while l_sum.shape[0] > 1:
        half = l_sum.shape[0] // 2
        got = xor_permute(l_sum[half:].astype(BF16), "col", n_col, half)
        l_sum = l_sum[:half] + got.astype(F32)
    grad_left = l_sum.reshape(s_l, ti, chans).transpose(2, 0, 1)

    w_sum = row_sum[s_r:]
    step = 1
    while step < n_col:
        w_sum = w_sum + xor_permute(w_sum, "col", n_col, step)
        step *= 2
    own_c = chans // n_row
    fold = wide // (2 * e)
    grad_weight = w_sum.reshape(w_rows, fold, 2, e).transpose(1, 0, 2, 3)
    grad_weight = (
        grad_weight.reshape(pairs, own_c, 2, e).transpose(1, 0, 2, 3).reshape(own_c * chans, e)
    )
    return grad_left, grad_right, grad_weight


def solution(mesh):
    return jax.shard_map(
        functools.partial(body, mesh.shape["row"], mesh.shape["col"]),
        mesh=mesh,
        in_specs=(P(None, "col", "row"), P(None, "row", "col"), P("row", "col", None), P()),
        out_specs=(P(None, "col", "row"), P(None, "row", "col"), P("row", None)),
        check_vma=False,
    )
```

```python
import functools

import jax
import jax.numpy as jnp
from jax import lax
from jax.experimental import pallas as pl
from jax.experimental.pallas import tpu as pltpu
from jax.sharding import PartitionSpec as P


F32 = jnp.float32
BF16 = jnp.bfloat16
STEPS = 4
VMEM = pl.BlockSpec(memory_space=pltpu.VMEM)
HBM = pl.BlockSpec(memory_space=pltpu.HBM)


def xor_permute(x, axis, size, k):
    return lax.ppermute(x, axis, [(r, r ^ k) for r in range(size)])


def near_slots(n_col):
    slots = [0]
    far = n_col // 2
    while far > 1:
        slots += [slot ^ far for slot in slots]
        far //= 2
    return slots


def prep_kernel(l_hbm, r_hbm, g_hbm, w_hbm, l_out, r_out, gbd_ref, wp, l_ref, r_ref, w_ref, sems):
    chans, _, ti = l_ref.shape
    tj = r_ref.shape[2]
    e = g_hbm.shape[2]
    pairs = chans // 2
    copies = [
        pltpu.make_async_copy(r_hbm, r_ref, sems.at[0]),
        pltpu.make_async_copy(l_hbm, l_ref, sems.at[1]),
        pltpu.make_async_copy(w_hbm, w_ref, sems.at[2]),
        pltpu.make_async_copy(g_hbm, gbd_ref.at[:, 0, :, pl.ds(0, e)], sems.at[3]),
        pltpu.make_async_copy(g_hbm, gbd_ref.at[:, 1, :, pl.ds(e, e)], sems.at[4]),
    ]
    for copy in copies:
        copy.start()
    zero = jnp.zeros((gbd_ref.shape[0], tj, e), BF16)
    gbd_ref[:, 0, :, e:] = zero
    gbd_ref[:, 1, :, :e] = zero
    copies[0].wait()
    per = 128 // tj
    for m in range(chans // per):
        r_out[:, m * 128 : (m + 1) * 128] = jnp.concatenate(
            [r_ref[m * per + k].astype(F32) for k in range(per)], axis=1
        ).astype(BF16)
    copies[1].wait()
    per = 128 // ti
    for m in range(chans // per):
        l_out[0, :, m * 128 : (m + 1) * 128] = jnp.concatenate(
            [l_ref[m * per + k].astype(F32) for k in range(per)], axis=1
        ).astype(BF16)
    copies[2].wait()
    swapped = jnp.swapaxes(w_ref[...].astype(F32).reshape(chans, chans, e), 0, 1).astype(BF16)
    for p in range(pairs):
        for d2 in range(2):
            wp[p * chans : (p + 1) * chans, d2 * e : (d2 + 1) * e] = swapped[2 * p + d2]
    copies[3].wait()
    copies[4].wait()


def outer_grad_kernel(gbd_ref, wp, y_ref):
    ti, _, tj, two_e = gbd_ref.shape
    lanes = 2 * tj
    pairs = y_ref.shape[1] // lanes
    chans = 2 * pairs
    for q in range(ti // 2):
        res = lax.dot_general(
            wp[...],
            gbd_ref[2 * q : 2 * q + 2].reshape(2 * lanes, two_e),
            (((1,), (1,)), ((), ())),
            preferred_element_type=F32,
        ).astype(BF16)
        for i in range(2):
            row = (2 * q + i) * chans
            for p in range(pairs):
                y_ref[row : row + chans, p * lanes : (p + 1) * lanes] = res[
                    p * chans : (p + 1) * chans, i * lanes : (i + 1) * lanes
                ]


def left_kernel(n_row, n_col, *refs):
    chips = n_row // 2
    r_refs = refs[:chips]
    y_ref, r_all, l_keep, l_mid, l_send, rblk, l_part = refs[chips:]
    row = lax.axis_index("row")
    col = lax.axis_index("col")
    core = row % 2
    chip = row // 2
    _, s_l, tall = l_keep.shape
    half = n_col // 2
    scale = 1.0 / (s_l * n_col)
    for k in range(chips):
        rblk[2 * k] = r_refs[k][0]
        rblk[2 * k + 1] = r_refs[k][1]
    r_all[...] = jnp.concatenate(
        [rblk[2 * ((p // 2) ^ chip) + ((p % 2) ^ core)] for p in range(n_row)], axis=0
    )
    span = tall // 4
    for n in range(4):
        res = lax.dot_general(
            r_all[...],
            y_ref[n * span : (n + 1) * span, :],
            (((1,), (1,)), ((), ())),
            preferred_element_type=F32,
        )
        for p in range(n_col):
            l_part[p ^ col, :, n * span : (n + 1) * span] = res[p * s_l : (p + 1) * s_l, :]
    for a in range(half // 2):
        l_keep[a] = l_part[4 * a]
        l_mid[a] = l_part[4 * a + 2]
        l_send[a] = (l_part[4 * a + 1] * scale).astype(BF16)
        l_send[half // 2 + a] = (l_part[4 * a + 3] * scale).astype(BF16)


def main_kernel(n_row, n_col, chans, *refs):
    l_near, l_far, r_all, gbd_ref, y_ref, keep_ref, send_ref = refs[:7]
    lblk, l_all, lt, x_ref, both = refs[7:]
    row = lax.axis_index("row")
    col = lax.axis_index("col")
    core = row % 2
    chip = row // 2
    _, _, tall = l_near.shape
    total, wide = r_all.shape
    s_r = total // n_row
    scale = 1.0 / total
    pairs = chans // 2
    lanes = wide // pairs
    ti = tall // chans
    per = ti // STEPS
    rows = per * chans
    two_e = gbd_ref.shape[3]
    own_c = chans // n_row

    for a, slot in enumerate(near_slots(n_col)):
        lblk[slot] = l_near[a]
        lblk[slot ^ 1] = l_far[a]
    by_chan = jnp.concatenate([lblk[p ^ col] for p in range(n_col)], axis=0).astype(F32).T
    lt[...] = (
        jnp.swapaxes(by_chan.reshape(chans, ti, total), 0, 1).reshape(tall, total).astype(BF16)
    )
    l_all[...] = lt[...].T
    tile = 2 * lanes

    def outer_step(n, carry):
        right = r_all[:, n * tile : (n + 1) * tile]
        for s in range(STEPS):
            res = jnp.dot(
                lt[s * rows : (s + 1) * rows, :], right, preferred_element_type=F32
            ).astype(BF16)
            for p in range(2):
                at = pl.ds((2 * n + p) * chans, chans)
                for i in range(per):
                    x_ref[at, (s * per + i) * lanes : (s * per + i + 1) * lanes] = res[
                        i * chans : (i + 1) * chans, p * lanes : (p + 1) * lanes
                    ]
        return carry

    for n in range(wide // tile):
        outer_step(n, 0)

    def place(r):
        return (r % 2) ^ core, (r // 2) ^ chip

    w_rows = pairs * own_c * two_e // wide
    height = pairs
    for first in range(0, pairs, height):
        res = jnp.dot(
            x_ref[first * chans : (first + height) * chans, :],
            gbd_ref[...].reshape(tall * wide // (pairs * chans), two_e),
            preferred_element_type=F32,
        ) * scale
        for r in range(n_row):
            piece = jnp.concatenate(
                [
                    res[p * chans + r * own_c : p * chans + (r + 1) * own_c, :]
                    for p in range(height)
                ],
                axis=0,
            )
            side, slot = place(r)
            for a in range(height * own_c // w_rows):
                at = first * own_c // w_rows + a
                both[side, slot, s_r : s_r + w_rows, at * two_e : (at + 1) * two_e] = piece[
                    a * w_rows : (a + 1) * w_rows, :
                ]

    span = wide // 4
    for n in range(4):
        res = (
            jnp.dot(
                l_all[...], y_ref[:, n * span : (n + 1) * span], preferred_element_type=F32
            )
            * scale
        )
        for r in range(n_row):
            side, slot = place(r)
            both[side, slot, :s_r, n * span : (n + 1) * span] = res[r * s_r : (r + 1) * s_r, :]
    keep_ref[...] = both[0]
    send_ref[...] = both[1]


def work(n_row, n_col, left_act, right_act, cotangent, weight):
    chans, s_l, ti = left_act.shape
    _, s_r, tj = right_act.shape
    e = cotangent.shape[2]
    chips = n_row // 2
    total = s_l * n_col
    pairs = chans // 2
    wide = chans * tj
    tall = chans * ti

    l_near, r_own, gbd, w_pairs = pl.pallas_call(
        prep_kernel,
        in_specs=[HBM] * 4,
        out_specs=[VMEM] * 4,
        out_shape=[
            jax.ShapeDtypeStruct((1, s_l, tall), BF16),
            jax.ShapeDtypeStruct((s_r, wide), BF16),
            jax.ShapeDtypeStruct((ti, 2, tj, 2 * e), BF16),
            jax.ShapeDtypeStruct((pairs * chans, 2 * e), BF16),
        ],
        scratch_shapes=[
            pltpu.VMEM((chans, s_l, ti), BF16),
            pltpu.VMEM((chans, s_r, tj), BF16),
            pltpu.VMEM((chans * chans, e), BF16),
            pltpu.SemaphoreType.DMA((5,)),
        ],
        compiler_params=pltpu.CompilerParams(vmem_limit_bytes=16 << 20),
    )(*[
        pltpu.with_memory_space_constraint(item, pltpu.HBM)
        for item in (left_act, right_act, cotangent, weight)
    ])
    r_other = xor_permute(r_own, "row", n_row, 1)
    half = n_col // 2
    far = half
    while far > 1:
        l_new = xor_permute(l_near, "col", n_col, far)
        l_near = jnp.concatenate([l_near, l_new])
        far //= 2
    r_pair = jnp.stack([r_own, r_other])
    r_set = [r_pair] + [xor_permute(r_pair, "row", n_row, 2 * k) for k in range(1, chips)]
    l_far = xor_permute(l_near, "col", n_col, 1)

    y = pl.pallas_call(
        outer_grad_kernel,
        in_specs=[VMEM] * 2,
        out_specs=VMEM,
        out_shape=jax.ShapeDtypeStruct((tall, wide), BF16),
        compiler_params=pltpu.CompilerParams(vmem_limit_bytes=16 << 20),
        cost_estimate=pl.CostEstimate(
            flops=4 * ti * tj * e * chans * chans, bytes_accessed=8 << 20, transcendentals=0
        ),
    )(gbd, w_pairs)

    w_rows = chans * chans * e // n_row // wide
    high = s_r + w_rows
    r_all, l_own, l_mid, l_send = pl.pallas_call(
        functools.partial(left_kernel, n_row, n_col),
        in_specs=[VMEM] * (chips + 1),
        out_specs=[VMEM] * 4,
        out_shape=[jax.ShapeDtypeStruct((total, wide), BF16)]
        + [jax.ShapeDtypeStruct((half // 2, s_l, tall), F32)] * 2
        + [jax.ShapeDtypeStruct((half, s_l, tall), BF16)],
        scratch_shapes=[
            pltpu.VMEM((n_row, s_r, wide), BF16),
            pltpu.VMEM((n_col, s_l, tall), F32),
        ],
        compiler_params=pltpu.CompilerParams(vmem_limit_bytes=16 << 20),
        cost_estimate=pl.CostEstimate(
            flops=2 * total * tall * wide, bytes_accessed=4 << 20, transcendentals=0
        ),
    )(*r_set, y)

    keep, send = pl.pallas_call(
        functools.partial(main_kernel, n_row, n_col, chans),
        in_specs=[VMEM] * 5,
        out_specs=[VMEM] * 2,
        out_shape=[jax.ShapeDtypeStruct((chips, high, wide), F32)] * 2,
        scratch_shapes=[
            pltpu.VMEM((n_col, s_l, tall), BF16),
            pltpu.VMEM((total, tall), BF16),
            pltpu.VMEM((tall, total), BF16),
            pltpu.VMEM((pairs * chans, 2 * ti * tj), BF16),
            pltpu.VMEM((2, chips, high, wide), F32),
        ],
        compiler_params=pltpu.CompilerParams(vmem_limit_bytes=24 << 20),
        cost_estimate=pl.CostEstimate(
            flops=6 * total * tall * wide, bytes_accessed=8 << 20, transcendentals=0
        ),
    )(l_near, l_far, r_all, gbd, y)

    other = xor_permute(send, "row", n_row, 1)
    l_got = xor_permute(l_send, "col", n_col, 1)
    l_mid = lax.optimization_barrier(l_mid * (1.0 / total))
    summed = keep + other
    row_sum = summed[0]
    got = [xor_permute(summed[k].astype(BF16), "row", n_row, 2 * k) for k in range(1, chips)]
    for item in got:
        row_sum = row_sum + item.astype(F32)

    part = half // 2
    l_new = xor_permute((l_mid + l_got[part:].astype(F32)).astype(BF16), "col", n_col, 2)
    l_own = lax.optimization_barrier(l_own * (1.0 / total))
    l_sum = l_own + l_got[:part].astype(F32) + l_new.astype(F32)
    far = 4
    while far < n_col:
        l_new = xor_permute(l_sum[1::2].astype(BF16), "col", n_col, far)
        l_sum = l_sum[0::2] + l_new.astype(F32)
        far *= 2

    r_sum, w_sum = lax.optimization_barrier((row_sum[:s_r], row_sum[s_r:]))
    far = 1
    while 2 * far < n_col:
        w_sum = w_sum + xor_permute(w_sum, "col", n_col, far)
        far *= 2
    w_own = w_sum.astype(BF16)
    w_sum = w_own.astype(F32) + xor_permute(w_own, "col", n_col, far).astype(F32)
    grad_right = r_sum.reshape(s_r, chans, tj).transpose(1, 0, 2)
    grad_left = l_sum.reshape(s_l, ti, chans).transpose(2, 0, 1)
    own_c = chans // n_row
    fold = wide // (2 * e)
    grad_weight = w_sum.reshape(w_rows, fold, 2, e).transpose(1, 0, 2, 3)
    grad_weight = (
        grad_weight.reshape(pairs, own_c, 2, e).transpose(1, 0, 2, 3).reshape(own_c * chans, e)
    )
    return grad_left, grad_right, grad_weight


def solution(mesh):
    return jax.shard_map(
        functools.partial(work, mesh.shape["row"], mesh.shape["col"]),
        mesh=mesh,
        in_specs=(P(None, "col", "row"), P(None, "row", "col"), P("row", "col", None), P()),
        out_specs=(P(None, "col", "row"), P(None, "row", "col"), P("row", None)),
        check_vma=False,
    )
```

```python
import functools

import jax
import jax.numpy as jnp
from jax import lax
from jax.experimental import pallas as pl
from jax.experimental.pallas import tpu as pltpu
from jax.sharding import PartitionSpec as P


F32 = jnp.float32
BF16 = jnp.bfloat16
STEPS = 4
VMEM = pl.BlockSpec(memory_space=pltpu.VMEM)
HBM = pl.BlockSpec(memory_space=pltpu.HBM)


def xor_permute(x, axis, size, k):
    return lax.ppermute(x, axis, [(r, r ^ k) for r in range(size)])


def near_slots(n_col):
    slots = [0]
    far = n_col // 2
    while far > 1:
        slots += [slot ^ far for slot in slots]
        far //= 2
    return slots


def prep_kernel(l_hbm, r_hbm, g_hbm, w_hbm, l_out, r_out, g_ref, w_ref, l_ref, r_ref, sems):
    chans, _, ti = l_ref.shape
    tj = r_ref.shape[2]
    copies = [
        pltpu.make_async_copy(r_hbm, r_ref, sems.at[0]),
        pltpu.make_async_copy(l_hbm, l_ref, sems.at[1]),
        pltpu.make_async_copy(w_hbm, w_ref, sems.at[2]),
        pltpu.make_async_copy(g_hbm, g_ref, sems.at[3]),
    ]
    for copy in copies:
        copy.start()
    copies[0].wait()
    per = 128 // tj
    for m in range(chans // per):
        r_out[:, m * 128 : (m + 1) * 128] = jnp.concatenate(
            [r_ref[m * per + k].astype(F32) for k in range(per)], axis=1
        ).astype(BF16)
    copies[1].wait()
    per = 128 // ti
    for m in range(chans // per):
        l_out[0, :, m * 128 : (m + 1) * 128] = jnp.concatenate(
            [l_ref[m * per + k].astype(F32) for k in range(per)], axis=1
        ).astype(BF16)
    copies[2].wait()
    copies[3].wait()


def outer_grad_kernel(g_ref, w_ref, y_ref, gbd_ref, wp):
    ti, tj, e = g_ref.shape
    lanes = 2 * tj
    pairs = y_ref.shape[1] // lanes
    chans = 2 * pairs
    zero = jnp.zeros((tj, e), BF16)
    swapped = jnp.swapaxes(w_ref[...].astype(F32).reshape(chans, chans, e), 0, 1).astype(BF16)
    for p in range(pairs):
        for d2 in range(2):
            wp[p * chans : (p + 1) * chans, d2 * e : (d2 + 1) * e] = swapped[2 * p + d2]
    for q in range(ti // 2):
        for i in (2 * q, 2 * q + 1):
            block = g_ref[i]
            gbd_ref[i, 0, :, :e] = block
            gbd_ref[i, 0, :, e:] = zero
            gbd_ref[i, 1, :, :e] = zero
            gbd_ref[i, 1, :, e:] = block
        res = lax.dot_general(
            wp[...],
            gbd_ref[2 * q : 2 * q + 2].reshape(2 * lanes, 2 * e),
            (((1,), (1,)), ((), ())),
            preferred_element_type=F32,
        ).astype(BF16)
        for i in range(2):
            row = (2 * q + i) * chans
            for p in range(pairs):
                y_ref[row : row + chans, p * lanes : (p + 1) * lanes] = res[
                    p * chans : (p + 1) * chans, i * lanes : (i + 1) * lanes
                ]


def left_kernel(n_row, n_col, *refs):
    chips = n_row // 2
    r_refs = refs[:chips]
    y_ref, r_all, l_keep, l_mid, l_send, rblk, l_part = refs[chips:]
    row = lax.axis_index("row")
    col = lax.axis_index("col")
    core = row % 2
    chip = row // 2
    _, s_l, tall = l_keep.shape
    half = n_col // 2
    scale = 1.0 / (s_l * n_col)
    for k in range(chips):
        rblk[2 * k] = r_refs[k][0]
        rblk[2 * k + 1] = r_refs[k][1]
    r_all[...] = jnp.concatenate(
        [rblk[2 * ((p // 2) ^ chip) + ((p % 2) ^ core)] for p in range(n_row)], axis=0
    )
    span = tall // 4
    for n in range(4):
        res = lax.dot_general(
            y_ref[n * span : (n + 1) * span, :],
            r_all[...],
            (((1,), (1,)), ((), ())),
            preferred_element_type=F32,
        ).T
        for p in range(n_col):
            l_part[p ^ col, :, n * span : (n + 1) * span] = res[p * s_l : (p + 1) * s_l, :]
    for a in range(half // 2):
        l_keep[a] = l_part[4 * a]
        l_mid[a] = l_part[4 * a + 2]
        l_send[a] = (l_part[4 * a + 1] * scale).astype(BF16)
        l_send[half // 2 + a] = (l_part[4 * a + 3] * scale).astype(BF16)


def main_kernel(n_row, n_col, chans, *refs):
    l_near, l_far, r_all, gbd_ref, y_ref, keep_ref, send_ref = refs[:7]
    lblk, l_all, lt, x_ref, both = refs[7:]
    row = lax.axis_index("row")
    col = lax.axis_index("col")
    core = row % 2
    chip = row // 2
    _, _, tall = l_near.shape
    total, wide = r_all.shape
    s_r = total // n_row
    scale = 1.0 / total
    pairs = chans // 2
    lanes = wide // pairs
    ti = tall // chans
    per = ti // STEPS
    rows = per * chans
    two_e = gbd_ref.shape[3]
    own_c = chans // n_row

    for a, slot in enumerate(near_slots(n_col)):
        lblk[slot] = l_near[a]
        lblk[slot ^ 1] = l_far[a]
    by_chan = jnp.concatenate([lblk[p ^ col] for p in range(n_col)], axis=0).astype(F32).T
    lt[...] = (
        jnp.swapaxes(by_chan.reshape(chans, ti, total), 0, 1).reshape(tall, total).astype(BF16)
    )
    l_all[...] = lt[...].T
    tile = 2 * lanes

    def outer_step(n, carry):
        right = r_all[:, n * tile : (n + 1) * tile]
        for s in range(STEPS):
            res = jnp.dot(
                lt[s * rows : (s + 1) * rows, :], right, preferred_element_type=F32
            ).astype(BF16)
            for p in range(2):
                at = pl.ds((2 * n + p) * chans, chans)
                for i in range(per):
                    x_ref[at, (s * per + i) * lanes : (s * per + i + 1) * lanes] = res[
                        i * chans : (i + 1) * chans, p * lanes : (p + 1) * lanes
                    ]
        return carry

    for n in range(wide // tile):
        outer_step(n, 0)

    def place(r):
        return (r % 2) ^ core, (r // 2) ^ chip

    w_rows = pairs * own_c * two_e // wide
    height = pairs
    for first in range(0, pairs, height):
        res = jnp.dot(
            x_ref[first * chans : (first + height) * chans, :],
            gbd_ref[...].reshape(tall * wide // (pairs * chans), two_e),
            preferred_element_type=F32,
        ) * scale
        for r in range(n_row):
            piece = jnp.concatenate(
                [
                    res[p * chans + r * own_c : p * chans + (r + 1) * own_c, :]
                    for p in range(height)
                ],
                axis=0,
            )
            side, slot = place(r)
            for a in range(height * own_c // w_rows):
                at = first * own_c // w_rows + a
                both[side, slot, s_r : s_r + w_rows, at * two_e : (at + 1) * two_e] = piece[
                    a * w_rows : (a + 1) * w_rows, :
                ]

    span = wide // 4
    for n in range(4):
        res = (
            jnp.dot(
                l_all[...], y_ref[:, n * span : (n + 1) * span], preferred_element_type=F32
            )
            * scale
        )
        for r in range(n_row):
            side, slot = place(r)
            both[side, slot, :s_r, n * span : (n + 1) * span] = res[r * s_r : (r + 1) * s_r, :]
    keep_ref[...] = both[0]
    send_ref[...] = both[1]


def work(n_row, n_col, left_act, right_act, cotangent, weight):
    chans, s_l, ti = left_act.shape
    _, s_r, tj = right_act.shape
    e = cotangent.shape[2]
    chips = n_row // 2
    total = s_l * n_col
    pairs = chans // 2
    wide = chans * tj
    tall = chans * ti

    l_near, r_own, g_near, w_near = pl.pallas_call(
        prep_kernel,
        in_specs=[HBM] * 4,
        out_specs=[VMEM] * 4,
        out_shape=[
            jax.ShapeDtypeStruct((1, s_l, tall), BF16),
            jax.ShapeDtypeStruct((s_r, wide), BF16),
            jax.ShapeDtypeStruct((ti, tj, e), BF16),
            jax.ShapeDtypeStruct((chans * chans, e), BF16),
        ],
        scratch_shapes=[
            pltpu.VMEM((chans, s_l, ti), BF16),
            pltpu.VMEM((chans, s_r, tj), BF16),
            pltpu.SemaphoreType.DMA((4,)),
        ],
        compiler_params=pltpu.CompilerParams(vmem_limit_bytes=16 << 20),
    )(*[
        pltpu.with_memory_space_constraint(item, pltpu.HBM)
        for item in (left_act, right_act, cotangent, weight)
    ])
    r_other = xor_permute(r_own, "row", n_row, 1)
    half = n_col // 2
    far = half
    while far > 1:
        l_new = xor_permute(l_near, "col", n_col, far)
        l_near = jnp.concatenate([l_near, l_new])
        far //= 2
    r_pair = jnp.stack([r_own, r_other])
    r_set = [r_pair]
    for k in range(1, chips):
        r_set.append(xor_permute(r_pair, "row", n_row, 2 * k))
    l_far = xor_permute(l_near, "col", n_col, 1)

    y, gbd = pl.pallas_call(
        outer_grad_kernel,
        in_specs=[VMEM] * 2,
        out_specs=[VMEM] * 2,
        out_shape=[
            jax.ShapeDtypeStruct((tall, wide), BF16),
            jax.ShapeDtypeStruct((ti, 2, tj, 2 * e), BF16),
        ],
        scratch_shapes=[pltpu.VMEM((pairs * chans, 2 * e), BF16)],
        compiler_params=pltpu.CompilerParams(vmem_limit_bytes=16 << 20),
        cost_estimate=pl.CostEstimate(
            flops=4 * ti * tj * e * chans * chans, bytes_accessed=8 << 20, transcendentals=0
        ),
    )(g_near, w_near)

    w_rows = chans * chans * e // n_row // wide
    high = s_r + w_rows
    r_all, l_own, l_mid, l_send = pl.pallas_call(
        functools.partial(left_kernel, n_row, n_col),
        in_specs=[VMEM] * (chips + 1),
        out_specs=[VMEM] * 4,
        out_shape=[jax.ShapeDtypeStruct((total, wide), BF16)]
        + [jax.ShapeDtypeStruct((half // 2, s_l, tall), F32)] * 2
        + [jax.ShapeDtypeStruct((half, s_l, tall), BF16)],
        scratch_shapes=[
            pltpu.VMEM((n_row, s_r, wide), BF16),
            pltpu.VMEM((n_col, s_l, tall), F32),
        ],
        compiler_params=pltpu.CompilerParams(vmem_limit_bytes=16 << 20),
        cost_estimate=pl.CostEstimate(
            flops=2 * total * tall * wide, bytes_accessed=4 << 20, transcendentals=0
        ),
    )(*r_set, y)

    keep, send = pl.pallas_call(
        functools.partial(main_kernel, n_row, n_col, chans),
        in_specs=[VMEM] * 5,
        out_specs=[VMEM] * 2,
        out_shape=[jax.ShapeDtypeStruct((chips, high, wide), F32)] * 2,
        scratch_shapes=[
            pltpu.VMEM((n_col, s_l, tall), BF16),
            pltpu.VMEM((total, tall), BF16),
            pltpu.VMEM((tall, total), BF16),
            pltpu.VMEM((pairs * chans, 2 * ti * tj), BF16),
            pltpu.VMEM((2, chips, high, wide), F32),
        ],
        compiler_params=pltpu.CompilerParams(vmem_limit_bytes=24 << 20),
        cost_estimate=pl.CostEstimate(
            flops=6 * total * tall * wide, bytes_accessed=8 << 20, transcendentals=0
        ),
    )(l_near, l_far, r_all, gbd, y)

    other = xor_permute(send, "row", n_row, 1)
    l_got = xor_permute(l_send, "col", n_col, 1)
    l_mid = lax.optimization_barrier(l_mid * (1.0 / total))
    summed = keep + other
    row_sum = summed[0]
    got = []
    for k in range(1, chips):
        got.append(xor_permute(summed[k].astype(BF16), "row", n_row, 2 * k))
    for item in got:
        row_sum = row_sum + item.astype(F32)

    part = half // 2
    l_new = xor_permute((l_mid + l_got[part:].astype(F32)).astype(BF16), "col", n_col, 2)
    l_own = lax.optimization_barrier(l_own * (1.0 / total))
    l_sum = l_own + l_got[:part].astype(F32) + l_new.astype(F32)
    far = 4
    while far < n_col:
        l_new = xor_permute(l_sum[1::2].astype(BF16), "col", n_col, far)
        l_sum = l_sum[0::2] + l_new.astype(F32)
        far *= 2

    r_sum, w_sum = lax.optimization_barrier((row_sum[:s_r], row_sum[s_r:]))
    far = 1
    while 2 * far < n_col:
        w_sum = w_sum + xor_permute(w_sum, "col", n_col, far)
        far *= 2
    w_own = w_sum.astype(BF16)
    w_sum = w_own.astype(F32) + xor_permute(w_own, "col", n_col, far).astype(F32)
    grad_right = r_sum.reshape(s_r, chans, tj).transpose(1, 0, 2)
    grad_left = l_sum.reshape(s_l, ti, chans).transpose(2, 0, 1)
    own_c = chans // n_row
    fold = wide // (2 * e)
    grad_weight = w_sum.reshape(w_rows, fold, 2, e).transpose(1, 0, 2, 3)
    grad_weight = (
        grad_weight.reshape(pairs, own_c, 2, e).transpose(1, 0, 2, 3).reshape(own_c * chans, e)
    )
    return grad_left, grad_right, grad_weight


def solution(mesh):
    return jax.shard_map(
        functools.partial(work, mesh.shape["row"], mesh.shape["col"]),
        mesh=mesh,
        in_specs=(P(None, "col", "row"), P(None, "row", "col"), P("row", "col", None), P()),
        out_specs=(P(None, "col", "row"), P(None, "row", "col"), P("row", None)),
        check_vma=False,
    )
```
